512 devices in a mesh: row: 32 (over x, z_lo, core), col: 16 (over z_hi, y).
Axes of the slice: x: 4, y: 4, z: 16 (z_hi: 4, z_lo: 4; z = z_hi * 4 + z_lo), core: 2. Of those that a mesh axis runs over, the one named last changes fastest.
Arguments:
- features: bfloat16 [65536, 512], P(('row', 'col')), may hold values from -6 to 6
- weight: bfloat16 [512, 512], replicated, may hold values from -0.25 to 0.25
- edge_tiles: bfloat16 [32, 16, 16, 3, 128, 128], P('row', 'col'), may hold values from -0.15625 to 0.15625
- tile_col: int32 [32, 16, 16, 3], P('row', 'col'), may hold values from 0 to 31, as said below
- tile_count: int32 [32, 16, 16], P('row', 'col'), may hold values from 0 to 3, as said below
- cotangent: bfloat16 [65536, 512], P(('row', 'col')), may hold values from -0.0234375 to 0.0234375
Outputs:
- activations: bfloat16 [65536, 512], P(('row', 'col'))
- weight_grad: float32 [512, 512], replicated
The draws below stay inside these ranges and needn't reach their ends.
Inputs may be any that keep to these rules, and one draw needn't show every extreme that they name: `tile_col`: the live slots of one row block name different column blocks; slots that are not live hold arbitrary column blocks. Slots 0 to tile_count - 1 of a row block are live; the others hold arbitrary edge weights that are not part of the adjacency. Some row block holds 3 live slots.
All inputs are finite; a program needn't handle non-finite values.
Results may differ from the reference program's by a relative error of at most 0.024.
Values may be sent and summed in bfloat16 or wider, within the bound.
A program may use at most 64 MiB of HBM per device.

```python
import jax
import jax.numpy as jnp
from jax import lax

F = 512
H = 512
BLK = 128
KR = 3
RBLK = 16
CBLK = 32
NODES = 65536


def draw_tile_count(key, part):
    base = jax.random.fold_in(key, 11)
    key_level, key_pick, key_cut, key_top = jax.random.split(base, 4)
    level = jax.random.randint(key_level, (CBLK, RBLK, 1), 1, KR + 1)
    picked = jax.random.randint(key_pick, (), 0, CBLK * RBLK)
    device_ids = jnp.arange(CBLK * RBLK, dtype=jnp.int32).reshape(CBLK, RBLK, 1)
    level = jnp.where(device_ids == picked, KR, level)
    cut = jax.random.randint(key_cut, (CBLK, RBLK, RBLK), 0, 4)
    count = level - cut * level // 6
    top_block = jax.random.randint(key_top, (CBLK, RBLK, 1), 0, RBLK)
    block_ids = jnp.arange(RBLK, dtype=jnp.int32)[None, None, :]
    count = jnp.where(block_ids == top_block, level, count)
    return count.astype(jnp.int32)


def draw_tile_col(key, part):
    base = jax.random.fold_in(key, 23)
    scores = jax.random.randint(base, (CBLK, RBLK, RBLK, CBLK), 0, 1 << 20)
    scores = scores * CBLK + jnp.arange(CBLK, dtype=jnp.int32)
    order = jnp.argsort(scores, axis=-1)
    return order[..., :KR].astype(jnp.int32)


def with_spikes(drawn, stream_key, source, target, shards_of, factor):
    def block_of(axis_at):
        return (jnp.arange(drawn.shape[axis_at]) // (drawn.shape[axis_at] // shards_of)).reshape((-1,) + (1,) * (drawn.ndim - 1 - axis_at))

    one_side = jax.random.permutation(stream_key, shards_of)[block_of(target)]
    other_side = (block_of(target) + shards_of // 2) % shards_of
    return jnp.where((block_of(source) == one_side) | (block_of(source) == other_side), factor * drawn, drawn)


def levels(own_key, shape, shards, least, high):
    loudness, own = 1.0, jax.random.fold_in(own_key, 6)
    for dim, parts in shards:
        draws = jnp.exp(jax.random.uniform(jax.random.fold_in(own, dim), (parts,), jnp.float32, least / len(shards), high / len(shards)))
        loudness = loudness * jnp.repeat(draws, shape[dim] // parts).reshape([-1 if axis == dim else 1 for axis in range(len(shape))])
    return loudness


def scatter_about(own_key, extent, deviation, most, cuts=(), kind=jnp.bfloat16):
    result = deviation * jax.random.normal(own_key, extent, jnp.float32)
    if cuts:
        result = result * levels(own_key, extent, cuts, -0.22, 0.18)
    return jnp.clip(result, -most, most).astype(kind)


def noise_with(key, dims, scale, bound, pieces, heavy, kind=jnp.bfloat16):
    result = scale * jax.random.normal(key, dims, jnp.float32)
    if pieces:
        result = result * levels(key, dims, pieces, -0.22, 0.18)
    return jnp.clip(with_spikes(result, jax.random.fold_in(key, 3), *heavy), -bound, bound).astype(kind)


def setup_inputs(seed: int = 0) -> dict:
    arg_keys = jax.random.split(jax.random.key(seed), 7)
    return {
        "features": scatter_about(arg_keys[0], (NODES, F), 1.0, 6.0, ((0, 512),)),
        "weight": scatter_about(arg_keys[1], (F, H), F ** -0.5, 0.25),
        "edge_tiles": noise_with(arg_keys[2], (CBLK, RBLK, RBLK, KR, BLK, BLK), (BLK * KR * RBLK // 2) ** -0.5, 0.15625, ((0, 32), (1, 16)), (1, 2, 16, 2.0)),
        "tile_col": draw_tile_col(jax.random.fold_in(arg_keys[6], 71), 0),
        "tile_count": draw_tile_count(jax.random.fold_in(arg_keys[6], 71), 0),
        "cotangent": scatter_about(arg_keys[5], (NODES, H), NODES ** -0.5, 0.0234375, ((0, 512),)),
    }


def reference(features, weight, edge_tiles, tile_col, tile_count, cotangent):
    node_blocks = features.reshape(CBLK * RBLK, BLK, F)

    def row_group(row_index):
        def one_entry(col_index):
            column_ids = tile_col[row_index, col_index] * RBLK + col_index
            picked = node_blocks[column_ids].astype(jnp.float32)
            is_live = jnp.arange(KR, dtype=jnp.int32)[None, :] < tile_count[row_index, col_index][:, None]
            masked = edge_tiles[row_index, col_index].astype(jnp.float32) * is_live[:, :, None, None].astype(jnp.float32)
            return jnp.einsum('akij,akjf->aif', masked, picked).astype(jnp.bfloat16)

        entry_terms = lax.map(one_entry, jnp.arange(RBLK, dtype=jnp.int32))
        return jnp.sum(entry_terms.astype(jnp.float32), axis=0).astype(jnp.bfloat16)

    aggregated = lax.map(row_group, jnp.arange(CBLK, dtype=jnp.int32)).reshape(NODES, F)
    preact = jnp.dot(aggregated, weight, preferred_element_type=jnp.float32)
    sigmoid_pre = jax.nn.sigmoid(preact)
    activations = (preact * sigmoid_pre).astype(jnp.bfloat16)
    pre_grad = (cotangent.astype(jnp.float32) * sigmoid_pre * (1.0 + preact * (1.0 - sigmoid_pre))).astype(jnp.bfloat16)
    weight_grad = jnp.dot(aggregated.T, pre_grad, preferred_element_type=jnp.float32)
    return activations, weight_grad
```

```python
import jax
import jax.numpy as jnp
from jax import lax
from jax.experimental import pallas as pl
from jax.experimental.pallas import tpu as pltpu
from jax.sharding import PartitionSpec as P

MESH = pl.DeviceIdType.MESH
BF, F32 = jnp.bfloat16, jnp.float32
N, W = 128, 512
CHUNKS = ((0, 128), (128, 128), (256, 128), (384, 128))
C = len(CHUNKS)


def device(x, zl, k, zh, y):
    return ((x * 4 + zl) * 2 + k, zh * 4 + y)


def turn(value, by):
    return lax.rem(value + (by + 16), 4)


def kernel(
    count_ref, col_ref, feat, edges, cot, weight, act_out, grad_out,
    *scratch,
):
    ag, te, r1, r2, su, sb, r3, r4 = (scratch[i * C : (i + 1) * C] for i in range(8))
    (raw, em, cv, wv, av, gv, own, sib, rsib, part, rxy, zown, rz, gz, gxy,
     in_sem, zs, zr, xs, xr, fs, fr, cs, cr, ys, yr, ys2, yr2, zs1, zr1, zs2, zr2, a_s, a_r) = scratch[8 * C :]
    row, col = lax.axis_index("row"), lax.axis_index("col")
    x, zl, k = row // 8, lax.rem(row // 2, 4), lax.rem(row, 2)
    zh, y = col // 4, lax.rem(col, 4)
    z = zh * 4 + zl
    sibling = device(x, zl, 1 - k, zh, y)

    def slot(core, at_x, at_zl=0):
        return core * 16 + at_x * 4 + at_zl

    def send(src, dst, send_sem, recv_sem, to):
        pltpu.make_async_remote_copy(
            src_ref=src, dst_ref=dst, send_sem=send_sem, recv_sem=recv_sem, device_id=to, device_id_type=MESH
        ).start()

    def wait(ref, sem):
        pltpu.make_async_copy(ref, ref, sem).wait()

    mine = slot(k, x, zl)
    loads = [
        pltpu.make_async_copy(feat.at[:, s : s + w], ag[f].at[mine], in_sem.at[f])
        for f, (s, w) in enumerate(CHUNKS)
    ]
    loads += [
        pltpu.make_async_copy(edges, raw, in_sem.at[C]),
        pltpu.make_async_copy(weight, wv, in_sem.at[C + 1]),
        pltpu.make_async_copy(cot, cv, in_sem.at[C + 2]),
    ]
    for load in loads:
        load.start()

    def xy_peer(i):
        return turn(x, i // 4), turn(y, i % 4)

    def z_peer(i):
        other = lax.rem(z + i, 16)
        return other

    barrier = pltpu.get_barrier_semaphore()
    pl.semaphore_signal(barrier, inc=1, device_id=sibling, device_id_type=MESH)
    for i in range(1, 16):
        px, py = xy_peer(i)
        pl.semaphore_signal(barrier, inc=1, device_id=device(px, zl, k, zh, py), device_id_type=MESH)
        pz = z_peer(i)
        pl.semaphore_signal(barrier, inc=1, device_id=device(x, lax.rem(pz, 4), k, pz // 4, y), device_id_type=MESH)
    pl.semaphore_wait(barrier, 31)

    right, left = device(turn(x, 1), zl, k, zh, y), device(turn(x, -1), zl, k, zh, y)

    def gather_z(f):
        loads[f].wait()
        for dz in range(1, 4):
            ref = ag[f].at[mine]
            send(ref, ref, zs.at[f], zr.at[f], device(x, turn(zl, dz), k, zh, y))

    def to_sibling(f, first, n):
        ref = ag[f].at[pl.ds(first, n)]
        send(ref, ref, cs.at[f], cr.at[f], sibling)

    def gather_x(f):
        wait(ag[f].at[pl.ds(0, 3)], zr.at[f])
        ref = ag[f].at[pl.ds(slot(k, x), 4)]
        send(ref, ref, xs.at[f], xr.at[f, 0], right)
        send(ref, ref, xs.at[f], xr.at[f, 1], left)
        to_sibling(f, slot(k, x), 4)

    def gather_on(f):
        lx, rx = turn(x, -1), turn(x, 1)
        wait(ag[f].at[pl.ds(0, 4)], xr.at[f, 0])
        ref = ag[f].at[pl.ds(slot(k, lx), 2)]
        send(ref, ref, fs.at[f], fr.at[f], right)
        wait(ag[f].at[pl.ds(0, 4)], xr.at[f, 1])
        ref = ag[f].at[pl.ds(slot(k, rx, 2), 2)]
        send(ref, ref, fs.at[f], fr.at[f], left)
        to_sibling(f, slot(k, lx), 4)
        to_sibling(f, slot(k, rx), 4)

    def gather_end(f):
        wait(ag[f].at[pl.ds(0, 4)], fr.at[f])
        to_sibling(f, slot(k, turn(x, 2)), 4)

    def mask_tiles():
        loads[C].wait()

        def one(a, _):
            count = count_ref[0, a]
            for s in range(3):
                tile = raw[a, s]
                em[a, :, s * N : (s + 1) * N] = jnp.where(s < count, tile, jnp.zeros_like(tile))
            return _

        lax.fori_loop(0, 16, one, 0)

    def terms(f, to_y):
        for q in range(4):
            a = q * 4 + to_y
            picked = []
            for s in range(3):
                j = col_ref[a, s]
                picked.append(ag[f][lax.rem(j, 2) * 16 + j // 2])
            made = jnp.dot(em[a], jnp.concatenate(picked, axis=0), preferred_element_type=F32)
            te[f][to_y * 4 + q] = made.astype(BF)

    up, down = device(x, zl, k, zh, turn(y, 1)), device(x, zl, k, zh, turn(y, -1))
    y_up, y_down, y_far = turn(y, 1), turn(y, -1), turn(y, 2)

    def multiply(f):
        wait(ag[f].at[pl.ds(0, 16)], cr.at[f])
        terms(f, y_far)
        send(te[f].at[pl.ds(y_far * 4, 2)], r1[f].at[0], ys.at[f], yr.at[f, 0], up)
        send(te[f].at[pl.ds(y_far * 4 + 2, 2)], r1[f].at[1], ys.at[f], yr.at[f, 1], down)
        terms(f, y_up)
        send(te[f].at[pl.ds(y_up * 4 + 2, 2)], r2[f].at[0, pl.ds(2, 2)], ys2.at[f], yr2.at[f], up)
        terms(f, y_down)
        send(te[f].at[pl.ds(y_down * 4, 2)], r2[f].at[1, pl.ds(0, 2)], ys2.at[f], yr2.at[f], down)
        terms(f, y)

    def reduce_y(f):
        wait(r1[f].at[0], yr.at[f, 0])
        at = pl.ds(y_up * 4, 2)
        te[f][at] = (te[f][at].astype(F32) + r1[f][0].astype(F32)).astype(BF)
        send(te[f].at[at], r2[f].at[0, pl.ds(0, 2)], ys2.at[f], yr2.at[f], up)
        wait(r1[f].at[1], yr.at[f, 1])
        at = pl.ds(y_down * 4 + 2, 2)
        te[f][at] = (te[f][at].astype(F32) + r1[f][1].astype(F32)).astype(BF)
        send(te[f].at[at], r2[f].at[1, pl.ds(2, 2)], ys2.at[f], yr2.at[f], down)

    z_up, z_down, z_far = turn(zh, 1), turn(zh, -1), turn(zh, 2)
    above, below = device(x, zl, k, z_up, y), device(x, zl, k, z_down, y)

    def reduce_y_end(f):
        wait(r2[f], yr2.at[f])

        def total(q):
            return te[f][y * 4 + q].astype(F32) + r2[f][0, q].astype(F32) + r2[f][1, q].astype(F32)

        sb[f][z_far] = total(z_far).astype(BF)
        send(sb[f].at[z_far, pl.ds(0, 64)], r3[f].at[0], zs1.at[f], zr1.at[f, 0], above)
        send(sb[f].at[z_far, pl.ds(64, 64)], r3[f].at[1], zs1.at[f], zr1.at[f, 1], below)
        for q in (z_up, z_down, zh):
            su[f][q] = total(q)

    def reduce_z(f):
        wait(r3[f].at[0], zr1.at[f, 0])
        sb[f][z_up, 0:64] = (su[f][z_up, 0:64] + r3[f][0].astype(F32)).astype(BF)
        sb[f][z_up, 64:128] = su[f][z_up, 64:128].astype(BF)
        send(sb[f].at[z_up], r4[f].at[0], zs2.at[f], zr2.at[f], above)
        wait(r3[f].at[1], zr1.at[f, 1])
        sb[f][z_down, 64:128] = (su[f][z_down, 64:128] + r3[f][1].astype(F32)).astype(BF)
        sb[f][z_down, 0:64] = su[f][z_down, 0:64].astype(BF)
        send(sb[f].at[z_down], r4[f].at[1], zs2.at[f], zr2.at[f], below)

    def reduce_z_end(f):
        wait(r4[f], zr2.at[f])
        s, w = CHUNKS[f]
        av[:, s : s + w] = (su[f][zh] + r4[f][0].astype(F32) + r4[f][1].astype(F32)).astype(BF)

    for f in range(C):
        gather_z(f)
    for t in range(C + 6):
        if t < C:
            gather_x(t)
        if t == 1:
            mask_tiles()
        if 0 <= t - 1 < C:
            gather_on(t - 1)
        if 0 <= t - 3 < C:
            reduce_y(t - 3)
        if 0 <= t - 4 < C:
            reduce_y_end(t - 4)
        if 0 <= t - 5 < C:
            reduce_z(t - 5)
        if 0 <= t - 6 < C:
            reduce_z_end(t - 6)
        if 0 <= t - 2 < C:
            gather_end(t - 2)
            multiply(t - 2)

    loads[C + 1].wait()
    loads[C + 2].wait()
    preact = jnp.dot(av[...], wv[...], preferred_element_type=F32)
    sig = jax.nn.sigmoid(preact)
    gv[...] = (cv[...].astype(F32) * sig * (1.0 + preact * (1.0 - sig))).astype(BF)
    act_out[...] = (preact * sig).astype(BF)

    def share(half):
        rows = av[:, pl.ds(pl.multiple_of(half * 256, 256), 256)]
        made = lax.dot_general(rows, gv[...], (((0,), (0,)), ((), ())), preferred_element_type=F32)
        return made.reshape(16, 16, W)

    sib[...] = share(1 - k).astype(BF)
    send(sib, rsib, a_s.at[0], a_r.at[0], sibling)
    own[...] = share(k)
    wait(rsib, a_r.at[0])
    own[...] = own[...] + rsib[...].astype(F32)
    part[...] = own[...].astype(BF)

    place = x * 4 + y
    for i in range(1, 16):
        px, py = xy_peer(i)
        send(part.at[px * 4 + py], rxy.at[i - 1], a_s.at[1], a_r.at[1], device(px, zl, k, zh, py))
    wait(rxy, a_r.at[1])
    total = own[place]
    for i in range(15):
        total = total + rxy[i].astype(F32)

    for q in range(4):
        zown[:, q, :] = total[:, q * 128 : (q + 1) * 128]
    for i in range(1, 16):
        pz = z_peer(i)
        send(zown.at[pz], rz.at[i - 1], a_s.at[2], a_r.at[2], device(x, lax.rem(pz, 4), k, pz // 4, y))
    wait(rz, a_r.at[2])
    done = zown[z]
    for i in range(15):
        done = done + rz[i]

    gz[z] = done
    for i in range(1, 16):
        pz = z_peer(i)
        send(gz.at[z], gz.at[z], a_s.at[3], a_r.at[3], device(x, lax.rem(pz, 4), k, pz // 4, y))
    wait(gz.at[pl.ds(0, 15)], a_r.at[3])
    here = k * 16 + place
    for q in range(4):
        gxy[here, :, q * 128 : (q + 1) * 128] = gz[:, q, :].astype(BF)
    for i in range(1, 16):
        px, py = xy_peer(i)
        send(gxy.at[here], gxy.at[here], a_s.at[4], a_r.at[4], device(px, zl, k, zh, py))
    wait(gxy.at[pl.ds(0, 15)], a_r.at[4])
    ref = gxy.at[pl.ds(k * 16, 16)]
    send(ref, ref, a_s.at[5], a_r.at[5], sibling)

    for f in range(C):
        wait(ag[f].at[pl.ds(0, 3)], zs.at[f])
        wait(ag[f].at[pl.ds(0, 8)], xs.at[f])
        wait(ag[f].at[pl.ds(0, 4)], fs.at[f])
        wait(ag[f].at[pl.ds(0, 16)], cs.at[f])
        wait(te[f].at[pl.ds(0, 4)], ys.at[f])
        wait(te[f].at[pl.ds(0, 8)], ys2.at[f])
        wait(sb[f].at[0], zs1.at[f])
        wait(sb[f].at[pl.ds(0, 2)], zs2.at[f])
    wait(sib, a_s.at[0])
    wait(rxy, a_s.at[1])
    wait(rz, a_s.at[2])
    wait(gz.at[pl.ds(0, 15)], a_s.at[3])
    wait(gxy.at[pl.ds(0, 15)], a_s.at[4])
    wait(ref, a_s.at[5])
    wait(ref, a_r.at[5])
    grad_out[...] = gxy[...].reshape(W, W)


def local(features, weight, edge_tiles, tile_col, tile_count, cotangent):
    vm = pltpu.VMEM
    scratch = []
    for shape, kind in (
        ((32, N), BF), ((16, N), BF), ((2, 2, N), BF), ((2, 4, N), BF),
        ((4, N), F32), ((4, N), BF), ((2, 64), BF), ((2, N), BF),
    ):
        scratch += [vm((*shape, w), kind) for _, w in CHUNKS]
    scratch += [
        vm((16, 3, N, N), BF), vm((16, N, 3 * N), BF), vm((N, W), BF), vm((W, W), BF), vm((N, W), BF), vm((N, W), BF),
        vm((16, 16, W), F32), vm((16, 16, W), BF), vm((16, 16, W), BF), vm((16, 16, W), BF), vm((15, 16, W), BF),
        vm((16, 4, 128), F32), vm((15, 4, 128), F32), vm((16, 4, 128), F32), vm((32, 16, W), BF),
    ]
    dma = pltpu.SemaphoreType.DMA
    scratch += [
        dma((C + 3,)), dma((C,)), dma((C,)), dma((C,)), dma((C, 2)), dma((C,)), dma((C,)), dma((C,)), dma((C,)),
        dma((C,)), dma((C, 2)), dma((C,)), dma((C,)), dma((C,)), dma((C, 2)), dma((C,)), dma((C,)), dma((6,)), dma((6,)),
    ]
    smem, any_, vmem = (pl.BlockSpec(memory_space=m) for m in (pltpu.SMEM, pl.ANY, pltpu.VMEM))
    activations, grad = pl.pallas_call(
        kernel,
        name="conv",
        out_shape=(jax.ShapeDtypeStruct((N, W), BF), jax.ShapeDtypeStruct((W, W), BF)),
        in_specs=[smem, smem, any_, any_, any_, any_],
        out_specs=(vmem, vmem),
        scratch_shapes=scratch,
        compiler_params=pltpu.CompilerParams(
            collective_id=0, has_side_effects=True, vmem_limit_bytes=40 * 2**20
        ),
    )(tile_count[0], tile_col[0, 0], features, edge_tiles[0, 0], cotangent, weight)
    return activations, grad.astype(F32)


def solution(mesh):
    return jax.shard_map(
        local,
        mesh=mesh,
        in_specs=(
            P(("row", "col"), None),
            P(),
            P("row", "col", None, None, None, None),
            P("row", "col", None, None),
            P("row", "col", None),
            P(("row", "col"), None),
        ),
        out_specs=(P(("row", "col"), None), P()),
        check_vma=False,
    )
```

```python
import jax
import jax.numpy as jnp
from jax import lax
from jax.experimental import pallas as pl
from jax.experimental.pallas import tpu as pltpu
from jax.sharding import PartitionSpec as P

MESH = pl.DeviceIdType.MESH
BF, F32 = jnp.bfloat16, jnp.float32
N, W = 128, 512
CHUNKS = ((0, 128), (128, 128), (256, 128), (384, 128))
C = len(CHUNKS)
PIECES = ((0, 0, 128), (1, 0, 128), (2, 0, 128), (3, 0, 64), (3, 64, 64))
NP = len(PIECES)
ORDER = (
    ("own", 0), ("own", 1), ("own", 2), ("own", 3), ("line", 0), ("line", 1), ("on", 0, 0), ("on", 1, 0),
    ("ring", 0, 1), ("on", 2, 0), ("on", 3, 0), ("ring", 0, 2), ("line", 2), ("end", 0, 0), ("ring", 1, 1),
    ("end", 1, 0), ("ring", 0, 3), ("on", 0, 1), ("end", 2, 0), ("ring", 1, 2), ("line", 3), ("end", 3, 0),
    ("on", 0, 2), ("ring", 2, 1), ("ring", 1, 3), ("on", 1, 1), ("on", 0, 3), ("ring", 2, 2), ("end", 0, 1),
    ("on", 1, 2), ("ring", 3, 1), ("end", 0, 2), ("ring", 2, 3), ("on", 2, 1), ("on", 1, 3), ("ring", 3, 2),
    ("end", 1, 1), ("end", 0, 3), ("end", 1, 2), ("on", 2, 2), ("ring", 3, 3), ("mul", 0, 0), ("on", 3, 1),
    ("mul", 0, 1), ("on", 2, 3), ("mul", 0, 2), ("end", 2, 1), ("mul", 0, 3), ("end", 1, 3), ("on", 3, 2),
    ("end", 2, 2), ("mul", 1, 0), ("on", 3, 3), ("mul", 1, 1), ("end", 3, 1), ("mul", 1, 2), ("y", 0),
    ("end", 2, 3), ("mul", 1, 3), ("end", 3, 2), ("mul", 2, 0), ("mul", 2, 1), ("end", 3, 3), ("mul", 2, 2),
    ("mul", 2, 3), ("y", 1), ("mul", 3, 0), ("mul", 3, 1), ("mul", 3, 2), ("mul", 3, 3), ("y_end", 0), ("y", 2),
    ("y_end", 1), ("y", 3), ("y", 4), ("z", 0), ("y_end", 2), ("y_end", 3), ("y_end", 4), ("z", 1), ("z_end", 0),
    ("z", 2), ("z", 3), ("z", 4), ("z_end", 1), ("z_end", 2), ("z_end", 3), ("z_end", 4),
)


def device(x, zl, k, zh, y):
    return ((x * 4 + zl) * 2 + k, zh * 4 + y)


def turn(value, by):
    return lax.rem(value + (by + 16), 4)


def far(offset):
    dx, dy = offset // 4, offset % 4
    return min(dx, 4 - dx) + min(dy, 4 - dy)


NEAR_FIRST = sorted(range(1, 16), key=far)


def kernel(
    count_ref, col_ref, feat, edges, cot, weight, act_out, grad_out,
    *scratch,
):
    ag, te = scratch[:C], scratch[C : 2 * C]
    r1, r2, su, sb, r3, r4 = (scratch[2 * C + i * NP : 2 * C + (i + 1) * NP] for i in range(6))
    (raw, em, cv, wv, av, gv, own, sib, rsib, part, rxy, hi, lo, gxy,
     in_sem, zs, zr, xs, xr, fs, fr, cs, cr, ys, yr, ys2, yr2, zs1, zr1, zs2, zr2, a_s, a_r, g_r) = scratch[2 * C + 6 * NP :]
    row, col = lax.axis_index("row"), lax.axis_index("col")
    x, zl, k = row // 8, lax.rem(row // 2, 4), lax.rem(row, 2)
    zh, y = col // 4, lax.rem(col, 4)
    sibling = device(x, zl, 1 - k, zh, y)
    right, left = device(turn(x, 1), zl, k, zh, y), device(turn(x, -1), zl, k, zh, y)
    up, down = device(x, zl, k, zh, turn(y, 1)), device(x, zl, k, zh, turn(y, -1))
    above, below = device(x, zl, k, turn(zh, 1), y), device(x, zl, k, turn(zh, -1), y)
    line = [device(x, turn(zl, d), k, zh, y) for d in (1, 2, 3)]
    first, last = 1 + lax.rem(zl, 2), 3 * (1 - zl // 2)
    places = (zl, first, 6 - zl - first - last, last)

    def slot(core, at_x, at_zl=0):
        return core * 16 + at_x * 4 + at_zl

    def send(src, dst, send_sem, recv_sem, to):
        pltpu.make_async_remote_copy(
            src_ref=src, dst_ref=dst, send_sem=send_sem, recv_sem=recv_sem, device_id=to, device_id_type=MESH
        ).start()

    def wait(ref, sem):
        pltpu.make_async_copy(ref, ref, sem).wait()

    loads = [
        pltpu.make_async_copy(feat.at[:, s : s + w], ag[f].at[slot(k, x, zl)], in_sem.at[f])
        for f, (s, w) in enumerate(CHUNKS)
    ]
    loads += [
        pltpu.make_async_copy(edges, raw, in_sem.at[C]),
        pltpu.make_async_copy(weight, wv, in_sem.at[C + 1]),
        pltpu.make_async_copy(cot, cv, in_sem.at[C + 2]),
    ]
    for load in loads:
        load.start()

    barrier = pltpu.get_barrier_semaphore()
    partners = [*line, above, below, right, left, up, down, sibling]
    for to in partners:
        pl.semaphore_signal(barrier, inc=1, device_id=to, device_id_type=MESH)
    pl.semaphore_wait(barrier, len(partners))

    def to_ring(f, i):
        ref = ag[f].at[slot(k, x, places[i])]
        send(ref, ref, xs.at[f], xr.at[f, 0, i], right)
        send(ref, ref, xs.at[f], xr.at[f, 1, i], left)
        send(ref, ref, cs.at[f], cr.at[f], sibling)

    def gather_own(f):
        loads[f].wait()
        to_ring(f, 0)

    def gather_line(f):
        ref = ag[f].at[slot(k, x, zl)]
        for to in line:
            send(ref, ref, zs.at[f], zr.at[f, zl], to)

    def gather_ring(f, i):
        wait(ag[f].at[slot(k, x, places[i])], zr.at[f, places[i]])
        to_ring(f, i)

    def gather_on(f, i):
        refs = [ag[f].at[slot(k, turn(x, d), places[i])] for d in (-1, 1)]
        for d in (i % 2, 1 - i % 2):
            wait(refs[d], xr.at[f, d, i])
            if d == i % 2:
                send(refs[d], refs[d], fs.at[f], fr.at[f, i], left if d else right)
            send(refs[d], refs[d], cs.at[f], cr.at[f], sibling)

    def gather_end(f, i):
        ref = ag[f].at[slot(k, turn(x, 2), places[i])]
        wait(ref, fr.at[f, i])
        send(ref, ref, cs.at[f], cr.at[f], sibling)

    def mask_tiles():
        loads[C].wait()

        def one(a, _):
            count = count_ref[0, a]
            for s in range(3):
                tile = raw[a, s]
                em[a, :, s * N : (s + 1) * N] = jnp.where(s < count, tile, jnp.zeros_like(tile))
            return _

        lax.fori_loop(0, 16, one, 0)

    def terms(f, to_y):
        for q in range(4):
            a = q * 4 + to_y
            picked = []
            for s in range(3):
                j = col_ref[s, 0, a]
                picked.append(ag[f][lax.rem(j, 2) * 16 + j // 2])
            made = jnp.dot(em[a], jnp.concatenate(picked, axis=0), preferred_element_type=F32)
            te[f][to_y * 4 + q] = made.astype(BF)

    y_up, y_down, y_far = turn(y, 1), turn(y, -1), turn(y, 2)

    def multiply(f, group):
        if group == 0:
            wait(ag[f].at[pl.ds(0, 16)], cr.at[f])
        terms(f, (y_far, y_up, y_down, y)[group])
        for p, (chunk, r, n) in enumerate(PIECES):
            rows = pl.ds(r, n)
            if chunk != f:
                continue
            if group == 0:
                send(te[f].at[pl.ds(y_far * 4, 2), rows], r1[p].at[0], ys.at[p], yr.at[p, 0], up)
                send(te[f].at[pl.ds(y_far * 4 + 2, 2), rows], r1[p].at[1], ys.at[p], yr.at[p, 1], down)
            if group == 1:
                send(te[f].at[pl.ds(y_up * 4 + 2, 2), rows], r2[p].at[0, pl.ds(2, 2)], ys2.at[p], yr2.at[p], up)
            if group == 2:
                send(te[f].at[pl.ds(y_down * 4, 2), rows], r2[p].at[1, pl.ds(0, 2)], ys2.at[p], yr2.at[p], down)

    def reduce_y(p):
        f, r, n = PIECES[p]
        for d, at, to in ((0, y_up * 4, up), (1, y_down * 4 + 2, down)):
            wait(r1[p].at[d], yr.at[p, d])
            ref = te[f].at[pl.ds(at, 2), pl.ds(r, n)]
            ref[...] = (ref[...].astype(F32) + r1[p][d].astype(F32)).astype(BF)
            send(ref, r2[p].at[d, pl.ds(2 * d, 2)], ys2.at[p], yr2.at[p], to)

    z_up, z_down, z_far = turn(zh, 1), turn(zh, -1), turn(zh, 2)

    def reduce_y_end(p):
        f, r, n = PIECES[p]
        wait(r2[p], yr2.at[p])

        def total(q):
            return te[f][y * 4 + q, r : r + n].astype(F32) + r2[p][0, q].astype(F32) + r2[p][1, q].astype(F32)

        sb[p][z_far] = total(z_far).astype(BF)
        send(sb[p].at[z_far, pl.ds(0, n // 2)], r3[p].at[0], zs1.at[p], zr1.at[p, 0], above)
        send(sb[p].at[z_far, pl.ds(n // 2, n // 2)], r3[p].at[1], zs1.at[p], zr1.at[p, 1], below)
        for q in (z_up, z_down, zh):
            su[p][q] = total(q)

    def reduce_z(p):
        h = PIECES[p][2] // 2
        for d, at, to in ((0, z_up, above), (1, z_down, below)):
            wait(r3[p].at[d], zr1.at[p, d])
            add, keep = pl.ds(d * h, h), pl.ds((1 - d) * h, h)
            sb[p][at, add] = (su[p][at, add] + r3[p][d].astype(F32)).astype(BF)
            sb[p][at, keep] = su[p][at, keep].astype(BF)
            send(sb[p].at[at], r4[p].at[d], zs2.at[p], zr2.at[p], to)

    def sent():
        for f in range(C):
            wait(ag[f].at[pl.ds(0, 3)], zs.at[f])
            wait(ag[f].at[pl.ds(0, 8)], xs.at[f])
            wait(ag[f].at[pl.ds(0, 4)], fs.at[f])
            wait(ag[f].at[pl.ds(0, 16)], cs.at[f])
        for p in range(NP):
            wait(r1[p], ys.at[p])
            wait(r2[p], ys2.at[p])
            wait(r3[p], zs1.at[p])
            wait(r4[p], zs2.at[p])

    def reduce_z_end(p):
        f, r, n = PIECES[p]
        s, w = CHUNKS[f]
        if p == NP - 1:
            sent()
            loads[C + 1].wait()
            loads[C + 2].wait()
        wait(r4[p], zr2.at[p])
        av[r : r + n, s : s + w] = (su[p][zh] + r4[p][0].astype(F32) + r4[p][1].astype(F32)).astype(BF)

    steps = {
        "own": gather_own, "line": gather_line, "ring": gather_ring, "on": gather_on, "end": gather_end, "mul": multiply,
        "y": reduce_y, "y_end": reduce_y_end, "z": reduce_z, "z_end": reduce_z_end,
    }
    for step, *which in ORDER:
        if (step, *which) == ("on", 0, 0):
            mask_tiles()
        steps[step](*which)

    preact = jnp.dot(av[...], wv[...], preferred_element_type=F32)
    sig = jax.nn.sigmoid(preact)
    gv[...] = (cv[...].astype(F32) * sig * (1.0 + preact * (1.0 - sig))).astype(BF)
    act_out[...] = (preact * sig).astype(BF)

    def share(half):
        rows = av[:, pl.ds(pl.multiple_of(half * 256, 256), 256)]
        made = lax.dot_general(rows, gv[...], (((0,), (0,)), ((), ())), preferred_element_type=F32)
        return made.reshape(16, 16, W)

    sib[...] = share(1 - k).astype(BF)
    send(sib, rsib, a_s.at[0], a_r.at[0], sibling)
    own[...] = share(k)
    wait(rsib, a_r.at[0])
    own[...] = own[...] + rsib[...].astype(F32)
    part[...] = own[...].astype(BF)

    place = x * 4 + y

    def peer(i):
        return turn(x, i // 4), turn(y, i % 4)

    for i in reversed(NEAR_FIRST):
        px, py = peer(i)
        send(part.at[px * 4 + py], rxy.at[i - 1], a_s.at[1], a_r.at[1], device(px, zl, k, zh, py))
    wait(rxy, a_r.at[1])
    total = own[place]
    for i in range(15):
        total = total + rxy[i].astype(F32)

    def exchange(buf, at, stage, to):
        buf[at] = total.astype(BF)
        for d in (2, 1, 3):
            send(buf.at[at], buf.at[at], a_s.at[stage], a_r.at[stage], to(d))
        wait(buf.at[pl.ds(0, 3)], a_r.at[stage])
        return sum(buf[i].astype(F32) for i in range(4))

    total = exchange(hi, zh, 2, lambda d: device(x, zl, k, turn(zh, d), y))
    total = exchange(lo, zl, 3, lambda d: line[d - 1])

    here = k * 16 + place
    gxy[here] = total.astype(BF)
    send(gxy.at[here], gxy.at[here], a_s.at[5], a_r.at[5], sibling)
    for i in reversed(NEAR_FIRST):
        px, py = peer(i)
        send(gxy.at[here], gxy.at[here], a_s.at[4], g_r.at[i], device(px, zl, k, zh, py))
    for i in NEAR_FIRST:
        ref = gxy.at[k * 16 + turn(x, -(i // 4)) * 4 + turn(y, -(i % 4))]
        wait(ref, g_r.at[i])
        send(ref, ref, a_s.at[5], a_r.at[5], sibling)

    wait(sib, a_s.at[0])
    wait(rxy, a_s.at[1])
    wait(hi.at[pl.ds(0, 3)], a_s.at[2])
    wait(lo.at[pl.ds(0, 3)], a_s.at[3])
    wait(rxy, a_s.at[4])
    wait(part, a_s.at[5])
    wait(part, a_r.at[5])
    grad_out[...] = gxy[...].reshape(W, W)


def local(features, weight, edge_tiles, tile_col, tile_count, cotangent):
    vm = pltpu.VMEM
    scratch = []
    for rows in (32, 16):
        scratch += [vm((rows, N, w), BF) for _, w in CHUNKS]
    for shape, part, kind in (((2, 2), 1, BF), ((2, 4), 1, BF), ((4,), 1, F32), ((4,), 1, BF), ((2,), 2, BF), ((2,), 1, BF)):
        scratch += [vm((*shape, n // part, CHUNKS[f][1]), kind) for f, _, n in PIECES]
    scratch += [
        vm((16, 3, N, N), BF), vm((16, N, 3 * N), BF), vm((N, W), BF), vm((W, W), BF), vm((N, W), BF), vm((N, W), BF),
        vm((16, 16, W), F32), vm((16, 16, W), BF), vm((16, 16, W), BF), vm((16, 16, W), BF), vm((15, 16, W), BF),
        vm((4, 16, W), BF), vm((4, 16, W), BF), vm((32, 16, W), BF),
    ]
    for shape in (
        (C + 3,), (C,), (C, 4), (C,), (C, 2, 4), (C,), (C, 4), (C,), (C,),
        (NP,), (NP, 2), (NP,), (NP,), (NP,), (NP, 2), (NP,), (NP,), (6,), (6,), (16,),
    ):
        scratch.append(pltpu.SemaphoreType.DMA(shape))
    smem, any_, vmem = (pl.BlockSpec(memory_space=m) for m in (pltpu.SMEM, pl.ANY, pltpu.VMEM))
    activations, grad = pl.pallas_call(
        kernel,
        name="conv",
        out_shape=(jax.ShapeDtypeStruct((N, W), BF), jax.ShapeDtypeStruct((W, W), BF)),
        in_specs=[smem, smem, any_, any_, any_, any_],
        out_specs=(vmem, vmem),
        scratch_shapes=scratch,
        compiler_params=pltpu.CompilerParams(
            collective_id=0, has_side_effects=True, vmem_limit_bytes=60 * 2**20
        ),
    )(tile_count[0], jnp.transpose(tile_col, (0, 3, 1, 2))[0], features, edge_tiles[0, 0], cotangent, weight)
    return activations, grad.astype(F32)


def solution(mesh):
    return jax.shard_map(
        local,
        mesh=mesh,
        in_specs=(
            P(("row", "col"), None),
            P(),
            P("row", "col", None, None, None, None),
            P("row", "col", None, None),
            P("row", "col", None),
            P(("row", "col"), None),
        ),
        out_specs=(P(("row", "col"), None), P()),
        check_vma=False,
    )
```

```python
import jax
import jax.numpy as jnp
from jax import lax
from jax.experimental import pallas as pl
from jax.experimental.pallas import tpu as pltpu
from jax.sharding import PartitionSpec as P

MESH = pl.DeviceIdType.MESH
BF, F32 = jnp.bfloat16, jnp.float32
N, W = 128, 512
CHUNKS = ((0, 128), (128, 128), (256, 128), (384, 128))
C = len(CHUNKS)
PIECES = tuple((f, r, 64) for f in range(C) for r in (0, 64))
NP = len(PIECES)


def of(step, f, first=1):
    return [(step, f, i) for i in range(first, 4)]


def pieces(step, f):
    return [(step, p) for p in range(NP) if PIECES[p][0] == f]


def mixed(*lists):
    return [each[i] for i in range(max(map(len, lists))) for each in lists if i < len(each)]


ORDER = [
    ("own", 0), ("line", 0), ("own", 1), ("line", 1), ("own", 2), ("line", 2), ("own", 3), ("line", 3),
    ("on", 0, 0), ("on", 1, 0), ("on", 2, 0), ("on", 3, 0),
    *of("ring", 0), *of("ring", 1), *of("on", 0), *of("ring", 2), *of("on", 1), *of("ring", 3),
    *of("end", 0, 0), *mixed(of("mul", 0, 0), of("on", 2)), *of("end", 1, 0), *mixed(of("mul", 1, 0), of("on", 3)),
    *pieces("y", 0), *of("end", 2, 0), *of("mul", 2, 0), *pieces("y", 1), *pieces("y_end", 0),
    *of("end", 3, 0), *of("mul", 3, 0), *pieces("y", 2), *pieces("y_end", 1), *pieces("z", 0),
    *pieces("y", 3), *pieces("y_end", 2), *pieces("y_end", 3), *pieces("z", 1), *pieces("z_end", 0),
    *pieces("z", 2), *pieces("z", 3), *pieces("z_end", 1), *pieces("z_end", 2), *pieces("z_end", 3),
]


def device(x, zl, k, zh, y):
    return ((x * 4 + zl) * 2 + k, zh * 4 + y)


def turn(value, by):
    return lax.rem(value + (by + 16), 4)


def far(offset):
    dx, dy = offset // 4, offset % 4
    return min(dx, 4 - dx) + min(dy, 4 - dy)


NEAR_FIRST = sorted(range(1, 16), key=far)


def kernel(
    count_ref, col_ref, feat, edges, cot, weight, act_out, grad_out,
    *scratch,
):
    ag, te = scratch[:C], scratch[C : 2 * C]
    r1, r2, su, sb, r3, r4 = (scratch[2 * C + i * NP : 2 * C + (i + 1) * NP] for i in range(6))
    (raw, em, cv, wv, av, gv, own, sib, rsib, part, rxy, hi, lo, gxy,
     in_sem, zs, zr, xs, xr, fs, fr, cs, cr, ys, yr, ys2, yr2, zs1, zr1, zs2, zr2, a_s, a_r, g_r) = scratch[2 * C + 6 * NP :]
    row, col = lax.axis_index("row"), lax.axis_index("col")
    x, zl, k = row // 8, lax.rem(row // 2, 4), lax.rem(row, 2)
    zh, y = col // 4, lax.rem(col, 4)
    sibling = device(x, zl, 1 - k, zh, y)
    right, left = device(turn(x, 1), zl, k, zh, y), device(turn(x, -1), zl, k, zh, y)
    up, down = device(x, zl, k, zh, turn(y, 1)), device(x, zl, k, zh, turn(y, -1))
    above, below = device(x, zl, k, turn(zh, 1), y), device(x, zl, k, turn(zh, -1), y)
    line = [device(x, turn(zl, d), k, zh, y) for d in (1, 2, 3)]
    first, last = 1 + lax.rem(zl, 2), 3 * (1 - zl // 2)
    places = (zl, first, 6 - zl - first - last, last)

    def slot(core, at_x, at_zl=0):
        return core * 16 + at_x * 4 + at_zl

    def send(src, dst, send_sem, recv_sem, to):
        pltpu.make_async_remote_copy(
            src_ref=src, dst_ref=dst, send_sem=send_sem, recv_sem=recv_sem, device_id=to, device_id_type=MESH
        ).start()

    def wait(ref, sem):
        pltpu.make_async_copy(ref, ref, sem).wait()

    loads = [
        pltpu.make_async_copy(feat.at[:, s : s + w], ag[f].at[slot(k, x, zl)], in_sem.at[f])
        for f, (s, w) in enumerate(CHUNKS)
    ]
    loads += [
        pltpu.make_async_copy(edges, raw, in_sem.at[C]),
        pltpu.make_async_copy(weight, wv, in_sem.at[C + 1]),
        pltpu.make_async_copy(cot, cv, in_sem.at[C + 2]),
    ]
    for load in loads:
        load.start()

    barrier = pltpu.get_barrier_semaphore()
    partners = [*line, above, below, right, left, up, down, sibling]
    for to in partners:
        pl.semaphore_signal(barrier, inc=1, device_id=to, device_id_type=MESH)
    pl.semaphore_wait(barrier, len(partners))

    def to_sibling(f, at_x):
        ref = ag[f].at[pl.ds(slot(k, at_x), 4)]
        send(ref, ref, cs.at[f], cr.at[f], sibling)

    def to_ring(f, i):
        ref = ag[f].at[slot(k, x, places[i])]
        send(ref, ref, xs.at[f], xr.at[f, 0, i], right)
        send(ref, ref, xs.at[f], xr.at[f, 1, i], left)
        if i == 3:
            to_sibling(f, x)

    def gather_own(f):
        loads[f].wait()
        to_ring(f, 0)

    def gather_line(f):
        ref = ag[f].at[slot(k, x, zl)]
        for to in line:
            send(ref, ref, zs.at[f], zr.at[f, zl], to)

    def gather_ring(f, i):
        ref = ag[f].at[slot(k, x, places[i])]
        wait(ref, zr.at[f, places[i]])
        to_ring(f, i)

    def gather_on(f, i):
        refs = [ag[f].at[slot(k, turn(x, d), places[i])] for d in (-1, 1)]
        for d in (i % 2, 1 - i % 2):
            wait(refs[d], xr.at[f, d, i])
            if d == i % 2:
                send(refs[d], refs[d], fs.at[f], fr.at[f, i], left if d else right)
            if i == 3:
                to_sibling(f, turn(x, (-1, 1)[d]))

    def gather_end(f, i):
        ref = ag[f].at[slot(k, turn(x, 2), places[i])]
        wait(ref, fr.at[f, i])
        if i == 3:
            to_sibling(f, turn(x, 2))

    def mask_tiles():
        loads[C].wait()

        def one(a, _):
            count = count_ref[0, a]
            for s in range(3):
                tile = raw[a, s]
                em[a, :, s * N : (s + 1) * N] = jnp.where(s < count, tile, jnp.zeros_like(tile))
            return _

        lax.fori_loop(0, 16, one, 0)

    def terms(f, to_y):
        for q in range(4):
            a = q * 4 + to_y
            picked = []
            for s in range(3):
                j = col_ref[s, 0, a]
                picked.append(ag[f][lax.rem(j, 2) * 16 + j // 2])
            made = jnp.dot(em[a], jnp.concatenate(picked, axis=0), preferred_element_type=F32)
            te[f][to_y * 4 + q] = made.astype(BF)

    y_up, y_down, y_far = turn(y, 1), turn(y, -1), turn(y, 2)

    def multiply(f, group):
        if group == 0:
            wait(ag[f].at[pl.ds(0, 16)], cr.at[f])
        terms(f, (y_far, y_up, y_down, y)[group])
        for p, (chunk, r, n) in enumerate(PIECES):
            rows = pl.ds(r, n)
            if chunk != f:
                continue
            if group == 0:
                send(te[f].at[pl.ds(y_far * 4, 2), rows], r1[p].at[0], ys.at[p], yr.at[p, 0], up)
                send(te[f].at[pl.ds(y_far * 4 + 2, 2), rows], r1[p].at[1], ys.at[p], yr.at[p, 1], down)
            if group == 1:
                send(te[f].at[pl.ds(y_up * 4 + 2, 2), rows], r2[p].at[0, pl.ds(2, 2)], ys2.at[p], yr2.at[p], up)
            if group == 2:
                send(te[f].at[pl.ds(y_down * 4, 2), rows], r2[p].at[1, pl.ds(0, 2)], ys2.at[p], yr2.at[p], down)

    def reduce_y(p):
        f, r, n = PIECES[p]
        for d, at, to in ((0, y_up * 4, up), (1, y_down * 4 + 2, down)):
            wait(r1[p].at[d], yr.at[p, d])
            ref = te[f].at[pl.ds(at, 2), pl.ds(r, n)]
            ref[...] = (ref[...].astype(F32) + r1[p][d].astype(F32)).astype(BF)
            send(ref, r2[p].at[d, pl.ds(2 * d, 2)], ys2.at[p], yr2.at[p], to)

    z_up, z_down, z_far = turn(zh, 1), turn(zh, -1), turn(zh, 2)

    def reduce_y_end(p):
        f, r, n = PIECES[p]
        wait(r2[p], yr2.at[p])

        def total(q):
            return te[f][y * 4 + q, r : r + n].astype(F32) + r2[p][0, q].astype(F32) + r2[p][1, q].astype(F32)

        sb[p][z_far] = total(z_far).astype(BF)
        send(sb[p].at[z_far, pl.ds(0, n // 2)], r3[p].at[0], zs1.at[p], zr1.at[p, 0], above)
        send(sb[p].at[z_far, pl.ds(n // 2, n // 2)], r3[p].at[1], zs1.at[p], zr1.at[p, 1], below)
        for q in (z_up, z_down, zh):
            su[p][q] = total(q)

    def reduce_z(p):
        h = PIECES[p][2] // 2
        for d, at, to in ((0, z_up, above), (1, z_down, below)):
            wait(r3[p].at[d], zr1.at[p, d])
            add, keep = pl.ds(d * h, h), pl.ds((1 - d) * h, h)
            sb[p][at, add] = (su[p][at, add] + r3[p][d].astype(F32)).astype(BF)
            sb[p][at, keep] = su[p][at, keep].astype(BF)
            send(sb[p].at[at], r4[p].at[d], zs2.at[p], zr2.at[p], to)

    def sent():
        for f in range(C):
            wait(ag[f].at[pl.ds(0, 3)], zs.at[f])
            wait(ag[f].at[pl.ds(0, 8)], xs.at[f])
            wait(ag[f].at[pl.ds(0, 4)], fs.at[f])
            wait(ag[f].at[pl.ds(0, 16)], cs.at[f])
        for p in range(NP):
            wait(r1[p], ys.at[p])
            wait(r2[p], ys2.at[p])
            wait(r3[p], zs1.at[p])
            wait(r4[p], zs2.at[p])

    def reduce_z_end(p):
        f, r, n = PIECES[p]
        s, w = CHUNKS[f]
        if p == NP - 1:
            sent()
            loads[C + 1].wait()
            loads[C + 2].wait()
        wait(r4[p], zr2.at[p])
        av[r : r + n, s : s + w] = (su[p][zh] + r4[p][0].astype(F32) + r4[p][1].astype(F32)).astype(BF)

    steps = {
        "own": gather_own, "line": gather_line, "ring": gather_ring, "on": gather_on, "end": gather_end, "mul": multiply,
        "y": reduce_y, "y_end": reduce_y_end, "z": reduce_z, "z_end": reduce_z_end,
    }
    for step, *which in ORDER:
        if (step, *which) == ("on", 0, 0):
            mask_tiles()
        steps[step](*which)

    preact = jnp.dot(av[...], wv[...], preferred_element_type=F32)
    sig = jax.nn.sigmoid(preact)
    gv[...] = (cv[...].astype(F32) * sig * (1.0 + preact * (1.0 - sig))).astype(BF)
    act_out[...] = (preact * sig).astype(BF)

    def share(half):
        rows = av[:, pl.ds(pl.multiple_of(half * 256, 256), 256)]
        made = lax.dot_general(rows, gv[...], (((0,), (0,)), ((), ())), preferred_element_type=F32)
        return made.reshape(16, 16, W)

    sib[...] = share(1 - k).astype(BF)
    send(sib, rsib, a_s.at[0], a_r.at[0], sibling)
    own[...] = share(k)
    wait(rsib, a_r.at[0])
    own[...] = own[...] + rsib[...].astype(F32)
    part[...] = own[...].astype(BF)

    place = x * 4 + y

    def peer(i):
        return turn(x, i // 4), turn(y, i % 4)

    for i in reversed(NEAR_FIRST):
        px, py = peer(i)
        send(part.at[px * 4 + py], rxy.at[i - 1], a_s.at[1], a_r.at[1], device(px, zl, k, zh, py))
    wait(rxy, a_r.at[1])
    total = own[place]
    for i in range(15):
        total = total + rxy[i].astype(F32)

    def exchange(buf, at, stage, to):
        buf[at] = total.astype(BF)
        for d in (2, 1, 3):
            send(buf.at[at], buf.at[at], a_s.at[stage], a_r.at[stage], to(d))
        wait(buf.at[pl.ds(0, 3)], a_r.at[stage])
        return sum(buf[i].astype(F32) for i in range(4))

    total = exchange(hi, zh, 2, lambda d: device(x, zl, k, turn(zh, d), y))
    total = exchange(lo, zl, 3, lambda d: line[d - 1])

    here = k * 16 + place
    gxy[here] = total.astype(BF)
    send(gxy.at[here], gxy.at[here], a_s.at[5], a_r.at[5], sibling)
    for i in reversed(NEAR_FIRST):
        px, py = peer(i)
        send(gxy.at[here], gxy.at[here], a_s.at[4], g_r.at[i], device(px, zl, k, zh, py))
    for i in NEAR_FIRST:
        ref = gxy.at[k * 16 + turn(x, -(i // 4)) * 4 + turn(y, -(i % 4))]
        wait(ref, g_r.at[i])
        send(ref, ref, a_s.at[5], a_r.at[5], sibling)

    wait(sib, a_s.at[0])
    wait(rxy, a_s.at[1])
    wait(hi.at[pl.ds(0, 3)], a_s.at[2])
    wait(lo.at[pl.ds(0, 3)], a_s.at[3])
    wait(rxy, a_s.at[4])
    wait(part, a_s.at[5])
    wait(part, a_r.at[5])
    grad_out[...] = gxy[...].reshape(W, W)


def local(features, weight, edge_tiles, tile_col, tile_count, cotangent):
    vm = pltpu.VMEM
    scratch = []
    for rows in (32, 16):
        scratch += [vm((rows, N, w), BF) for _, w in CHUNKS]
    for shape, part, kind in (((2, 2), 1, BF), ((2, 4), 1, BF), ((4,), 1, F32), ((4,), 1, BF), ((2,), 2, BF), ((2,), 1, BF)):
        scratch += [vm((*shape, n // part, CHUNKS[f][1]), kind) for f, _, n in PIECES]
    scratch += [
        vm((16, 3, N, N), BF), vm((16, N, 3 * N), BF), vm((N, W), BF), vm((W, W), BF), vm((N, W), BF), vm((N, W), BF),
        vm((16, 16, W), F32), vm((16, 16, W), BF), vm((16, 16, W), BF), vm((16, 16, W), BF), vm((15, 16, W), BF),
        vm((4, 16, W), BF), vm((4, 16, W), BF), vm((32, 16, W), BF),
    ]
    for shape in (
        (C + 3,), (C,), (C, 4), (C,), (C, 2, 4), (C,), (C, 4), (C,), (C,),
        (NP,), (NP, 2), (NP,), (NP,), (NP,), (NP, 2), (NP,), (NP,), (6,), (6,), (16,),
    ):
        scratch.append(pltpu.SemaphoreType.DMA(shape))
    smem, hbm, vmem = (pl.BlockSpec(memory_space=m) for m in (pltpu.SMEM, pltpu.HBM, pltpu.VMEM))
    activations, grad = pl.pallas_call(
        kernel,
        name="conv",
        out_shape=(jax.ShapeDtypeStruct((N, W), BF), jax.ShapeDtypeStruct((W, W), BF)),
        in_specs=[smem, smem, hbm, hbm, hbm, hbm],
        out_specs=(vmem, vmem),
        scratch_shapes=scratch,
        compiler_params=pltpu.CompilerParams(
            collective_id=0, has_side_effects=True, vmem_limit_bytes=60 * 2**20
        ),
    )(tile_count[0], jnp.transpose(tile_col, (0, 3, 1, 2))[0], features, edge_tiles[0, 0], cotangent, weight)
    return activations, grad.astype(F32)


def solution(mesh):
    return jax.shard_map(
        local,
        mesh=mesh,
        in_specs=(
            P(("row", "col"), None),
            P(),
            P("row", "col", None, None, None, None),
            P("row", "col", None, None),
            P("row", "col", None),
            P(("row", "col"), None),
        ),
        out_specs=(P(("row", "col"), None), P()),
        check_vma=False,
    )
```

```python
import jax
import jax.numpy as jnp
from jax import lax
from jax.experimental import pallas as pl
from jax.experimental.pallas import tpu as pltpu
from jax.sharding import PartitionSpec as P

MESH = pl.DeviceIdType.MESH
BF, F32 = jnp.bfloat16, jnp.float32
N, W = 128, 512
CHUNKS = ((0, 128), (128, 128), (256, 128), (384, 128))
C = len(CHUNKS)
PIECES = tuple((f, r, 64) for f in range(C) for r in (0, 64))
NP = len(PIECES)


def of(step, f, first=1):
    return [(step, f, i) for i in range(first, 4)]


def pieces(step, f):
    return [(step, p) for p in range(NP) if PIECES[p][0] == f]


def mixed(*lists):
    return [each[i] for i in range(max(map(len, lists))) for each in lists if i < len(each)]


ORDER = [
    ("own", 0), ("line", 0), ("own", 1), ("line", 1), ("own", 2), ("line", 2), ("own", 3), ("line", 3),
    ("on", 0, 0), ("on", 1, 0), ("on", 2, 0), ("on", 3, 0),
    *of("ring", 0), *of("ring", 1), *of("on", 0), *of("ring", 2), *of("on", 1), *of("ring", 3),
    *of("end", 0, 0), *mixed(of("mul", 0, 0), of("on", 2)), *of("end", 1, 0), *mixed(of("mul", 1, 0), of("on", 3)),
    *pieces("y", 0), *of("end", 2, 0), *of("mul", 2, 0), *pieces("y", 1), *pieces("y_end", 0),
    *of("end", 3, 0), *of("mul", 3, 0), *pieces("y", 2), *pieces("y_end", 1), *pieces("z", 0),
    *pieces("y", 3), *pieces("y_end", 2), *pieces("y_end", 3), *pieces("z", 1), *pieces("z_end", 0),
    *pieces("z", 2), *pieces("z", 3), *pieces("z_end", 1), *pieces("z_end", 2), *pieces("z_end", 3),
]


def device(x, zl, k, zh, y):
    return ((x * 4 + zl) * 2 + k, zh * 4 + y)


def turn(value, by):
    return lax.rem(value + (by + 16), 4)


def far(offset):
    dx, dy = offset // 4, offset % 4
    return min(dx, 4 - dx) + min(dy, 4 - dy)


NEAR_FIRST = sorted(range(1, 16), key=far)


def kernel(
    count_ref, col_ref, feat, edges, cot, weight, act_out, grad_out,
    *scratch,
):
    ag, te = scratch[:C], scratch[C : 2 * C]
    r1, r2, su, sb, r3, r4 = (scratch[2 * C + i * NP : 2 * C + (i + 1) * NP] for i in range(6))
    (raw, em, cv, wv, av, gv, own, sib, rsib, part, rxy, hi, lo, gxy,
     in_sem, zs, zr, xs, xr, fs, fr, cs, cr, ys, yr, ys2, yr2, zs1, zr1, zs2, zr2, a_s, a_r, g_r) = scratch[2 * C + 6 * NP :]
    row, col = lax.axis_index("row"), lax.axis_index("col")
    x, zl, k = row // 8, lax.rem(row // 2, 4), lax.rem(row, 2)
    zh, y = col // 4, lax.rem(col, 4)
    sibling = device(x, zl, 1 - k, zh, y)
    right, left = device(turn(x, 1), zl, k, zh, y), device(turn(x, -1), zl, k, zh, y)
    up, down = device(x, zl, k, zh, turn(y, 1)), device(x, zl, k, zh, turn(y, -1))
    above, below = device(x, zl, k, turn(zh, 1), y), device(x, zl, k, turn(zh, -1), y)
    line = [device(x, turn(zl, d), k, zh, y) for d in (1, 2, 3)]
    first, last = 1 + lax.rem(zl, 2), 3 * (1 - zl // 2)
    places = (zl, first, 6 - zl - first - last, last)

    def slot(core, at_x, at_zl=0):
        return core * 16 + at_x * 4 + at_zl

    def send(src, dst, send_sem, recv_sem, to):
        pltpu.make_async_remote_copy(
            src_ref=src, dst_ref=dst, send_sem=send_sem, recv_sem=recv_sem, device_id=to, device_id_type=MESH
        ).start()

    def wait(ref, sem):
        pltpu.make_async_copy(ref, ref, sem).wait()

    loads = [
        pltpu.make_async_copy(feat.at[:, s : s + w], ag[f].at[slot(k, x, zl)], in_sem.at[f])
        for f, (s, w) in enumerate(CHUNKS)
    ]
    loads += [
        pltpu.make_async_copy(edges, raw, in_sem.at[C]),
        pltpu.make_async_copy(weight, wv, in_sem.at[C + 1]),
        pltpu.make_async_copy(cot, cv, in_sem.at[C + 2]),
    ]
    for load in loads:
        load.start()

    barrier = pltpu.get_barrier_semaphore()
    partners = [*line, above, below, right, left, up, down, sibling]
    for to in partners:
        pl.semaphore_signal(barrier, inc=1, device_id=to, device_id_type=MESH)
    pl.semaphore_wait(barrier, len(partners))

    def to_sibling(f, at_x):
        ref = ag[f].at[pl.ds(slot(k, at_x), 4)]
        send(ref, ref, cs.at[f], cr.at[f], sibling)

    def to_ring(f, i):
        ref = ag[f].at[slot(k, x, places[i])]
        send(ref, ref, xs.at[f], xr.at[f, 0, i], right)
        send(ref, ref, xs.at[f], xr.at[f, 1, i], left)
        if i == 3:
            to_sibling(f, x)

    def gather_own(f):
        loads[f].wait()
        to_ring(f, 0)

    def gather_line(f):
        ref = ag[f].at[slot(k, x, zl)]
        for to in line:
            send(ref, ref, zs.at[f], zr.at[f, zl], to)

    def gather_ring(f, i):
        ref = ag[f].at[slot(k, x, places[i])]
        wait(ref, zr.at[f, places[i]])
        to_ring(f, i)

    def gather_on(f, i):
        refs = [ag[f].at[slot(k, turn(x, d), places[i])] for d in (-1, 1)]
        for d in (i % 2, 1 - i % 2):
            wait(refs[d], xr.at[f, d, i])
            if d == i % 2:
                send(refs[d], refs[d], fs.at[f], fr.at[f, i], left if d else right)
            if i == 3:
                to_sibling(f, turn(x, (-1, 1)[d]))

    def gather_end(f, i):
        ref = ag[f].at[slot(k, turn(x, 2), places[i])]
        wait(ref, fr.at[f, i])
        if i == 3:
            to_sibling(f, turn(x, 2))

    def mask_tiles():
        loads[C].wait()

        def one(a, _):
            count = count_ref[0, a]
            for s in range(3):
                tile = raw[a, s]
                em[a, :, s * N : (s + 1) * N] = jnp.where(s < count, tile, jnp.zeros_like(tile))
            return _

        lax.fori_loop(0, 16, one, 0)

    def terms(f, to_y):
        for q in range(4):
            a = q * 4 + to_y
            picked = []
            for s in range(3):
                j = col_ref[s, 0, a]
                picked.append(ag[f][lax.rem(j, 2) * 16 + j // 2])
            made = jnp.dot(em[a], jnp.concatenate(picked, axis=0), preferred_element_type=F32)
            te[f][to_y * 4 + q] = made.astype(BF)

    y_up, y_down, y_far = turn(y, 1), turn(y, -1), turn(y, 2)

    def multiply(f, group):
        if group == 0:
            wait(ag[f].at[pl.ds(0, 16)], cr.at[f])
        terms(f, (y_far, y_up, y_down, y)[group])
        for p, (chunk, r, n) in enumerate(PIECES):
            rows = pl.ds(r, n)
            if chunk != f:
                continue
            if group == 0:
                send(te[f].at[pl.ds(y_far * 4, 2), rows], r1[p].at[0], ys.at[p], yr.at[p, 0], up)
                send(te[f].at[pl.ds(y_far * 4 + 2, 2), rows], r1[p].at[1], ys.at[p], yr.at[p, 1], down)
            if group == 1:
                send(te[f].at[pl.ds(y_up * 4 + 2, 2), rows], r2[p].at[0, pl.ds(2, 2)], ys2.at[p], yr2.at[p], up)
            if group == 2:
                send(te[f].at[pl.ds(y_down * 4, 2), rows], r2[p].at[1, pl.ds(0, 2)], ys2.at[p], yr2.at[p], down)

    def reduce_y(p):
        f, r, n = PIECES[p]
        for d, at, to in ((0, y_up * 4, up), (1, y_down * 4 + 2, down)):
            wait(r1[p].at[d], yr.at[p, d])
            ref = te[f].at[pl.ds(at, 2), pl.ds(r, n)]
            ref[...] = (ref[...].astype(F32) + r1[p][d].astype(F32)).astype(BF)
            send(ref, r2[p].at[d, pl.ds(2 * d, 2)], ys2.at[p], yr2.at[p], to)

    z_up, z_down, z_far = turn(zh, 1), turn(zh, -1), turn(zh, 2)

    def reduce_y_end(p):
        f, r, n = PIECES[p]
        wait(r2[p], yr2.at[p])

        def total(q):
            return te[f][y * 4 + q, r : r + n].astype(F32) + r2[p][0, q].astype(F32) + r2[p][1, q].astype(F32)

        sb[p][z_far] = total(z_far).astype(BF)
        send(sb[p].at[z_far, pl.ds(0, n // 2)], r3[p].at[0], zs1.at[p], zr1.at[p, 0], above)
        send(sb[p].at[z_far, pl.ds(n // 2, n // 2)], r3[p].at[1], zs1.at[p], zr1.at[p, 1], below)
        for q in (z_up, z_down, zh):
            su[p][q] = total(q)

    def reduce_z(p):
        h = PIECES[p][2] // 2
        for d, at, to in ((0, z_up, above), (1, z_down, below)):
            wait(r3[p].at[d], zr1.at[p, d])
            add, keep = pl.ds(d * h, h), pl.ds((1 - d) * h, h)
            sb[p][at, add] = (su[p][at, add] + r3[p][d].astype(F32)).astype(BF)
            sb[p][at, keep] = su[p][at, keep].astype(BF)
            send(sb[p].at[at], r4[p].at[d], zs2.at[p], zr2.at[p], to)

    def sent():
        for f in range(C):
            wait(ag[f].at[pl.ds(0, 3)], zs.at[f])
            wait(ag[f].at[pl.ds(0, 8)], xs.at[f])
            wait(ag[f].at[pl.ds(0, 4)], fs.at[f])
            wait(ag[f].at[pl.ds(0, 16)], cs.at[f])
        for p in range(NP):
            wait(r1[p], ys.at[p])
            wait(r2[p], ys2.at[p])
            wait(r3[p], zs1.at[p])
            wait(r4[p], zs2.at[p])

    def reduce_z_end(p):
        f, r, n = PIECES[p]
        s, w = CHUNKS[f]
        if p == NP - 1:
            sent()
            loads[C + 1].wait()
            loads[C + 2].wait()
        wait(r4[p], zr2.at[p])
        av[r : r + n, s : s + w] = (su[p][zh] + r4[p][0].astype(F32) + r4[p][1].astype(F32)).astype(BF)

    steps = {
        "own": gather_own, "line": gather_line, "ring": gather_ring, "on": gather_on, "end": gather_end, "mul": multiply,
        "y": reduce_y, "y_end": reduce_y_end, "z": reduce_z, "z_end": reduce_z_end,
    }
    for step, *which in ORDER:
        if (step, *which) == ("on", 0, 0):
            mask_tiles()
        steps[step](*which)

    preact = jnp.dot(av[...], wv[...], preferred_element_type=F32)
    sig = jax.nn.sigmoid(preact)
    gv[...] = (cv[...].astype(F32) * sig * (1.0 + preact * (1.0 - sig))).astype(BF)
    act_out[...] = (preact * sig).astype(BF)

    def share(half):
        rows = av[:, pl.ds(pl.multiple_of(half * 256, 256), 256)]
        made = lax.dot_general(rows, gv[...], (((0,), (0,)), ((), ())), preferred_element_type=F32)
        return made.reshape(16, 16, W)

    sib[...] = share(1 - k).astype(BF)
    send(sib, rsib, a_s.at[0], a_r.at[0], sibling)
    own[...] = share(k)
    wait(rsib, a_r.at[0])

    place = x * 4 + y

    def peer(i):
        return turn(x, i // 4), turn(y, i % 4)

    for i in reversed(NEAR_FIRST):
        px, py = peer(i)
        part[px * 4 + py] = (own[px * 4 + py] + rsib[px * 4 + py].astype(F32)).astype(BF)
        send(part.at[px * 4 + py], rxy.at[i - 1], a_s.at[1], a_r.at[1], device(px, zl, k, zh, py))
    wait(rxy, a_r.at[1])
    total = own[place] + rsib[place].astype(F32)
    for i in range(15):
        total = total + rxy[i].astype(F32)

    def exchange(buf, at, stage, to):
        buf[at] = total.astype(BF)
        for d in (2, 1, 3):
            send(buf.at[at], buf.at[at], a_s.at[stage], a_r.at[stage], to(d))
        wait(buf.at[pl.ds(0, 3)], a_r.at[stage])
        return sum(buf[i].astype(F32) for i in range(4))

    total = exchange(lo, zl, 3, lambda d: line[d - 1])
    total = exchange(hi, zh, 2, lambda d: device(x, zl, k, turn(zh, d), y))

    here = k * 16 + place
    gxy[here] = total.astype(BF)
    send(gxy.at[here], gxy.at[here], a_s.at[5], a_r.at[5], sibling)
    for i in reversed(NEAR_FIRST):
        px, py = peer(i)
        send(gxy.at[here], gxy.at[here], a_s.at[4], g_r.at[i], device(px, zl, k, zh, py))
    for i in NEAR_FIRST:
        ref = gxy.at[k * 16 + turn(x, -(i // 4)) * 4 + turn(y, -(i % 4))]
        wait(ref, g_r.at[i])
        send(ref, ref, a_s.at[5], a_r.at[5], sibling)

    wait(sib, a_s.at[0])
    wait(rxy, a_s.at[1])
    wait(hi.at[pl.ds(0, 3)], a_s.at[2])
    wait(lo.at[pl.ds(0, 3)], a_s.at[3])
    wait(rxy, a_s.at[4])
    wait(part, a_s.at[5])
    wait(part, a_r.at[5])
    grad_out[...] = gxy[...].reshape(W, W)


def local(features, weight, edge_tiles, tile_col, tile_count, cotangent):
    vm = pltpu.VMEM
    scratch = []
    for rows in (32, 16):
        scratch += [vm((rows, N, w), BF) for _, w in CHUNKS]
    for shape, part, kind in (((2, 2), 1, BF), ((2, 4), 1, BF), ((4,), 1, F32), ((4,), 1, BF), ((2,), 2, BF), ((2,), 1, BF)):
        scratch += [vm((*shape, n // part, CHUNKS[f][1]), kind) for f, _, n in PIECES]
    scratch += [
        vm((16, 3, N, N), BF), vm((16, N, 3 * N), BF), vm((N, W), BF), vm((W, W), BF), vm((N, W), BF), vm((N, W), BF),
        vm((16, 16, W), F32), vm((16, 16, W), BF), vm((16, 16, W), BF), vm((16, 16, W), BF), vm((15, 16, W), BF),
        vm((4, 16, W), BF), vm((4, 16, W), BF), vm((32, 16, W), BF),
    ]
    for shape in (
        (C + 3,), (C,), (C, 4), (C,), (C, 2, 4), (C,), (C, 4), (C,), (C,),
        (NP,), (NP, 2), (NP,), (NP,), (NP,), (NP, 2), (NP,), (NP,), (6,), (6,), (16,),
    ):
        scratch.append(pltpu.SemaphoreType.DMA(shape))
    smem, hbm, vmem = (pl.BlockSpec(memory_space=m) for m in (pltpu.SMEM, pltpu.HBM, pltpu.VMEM))
    activations, grad = pl.pallas_call(
        kernel,
        name="conv",
        out_shape=(jax.ShapeDtypeStruct((N, W), BF), jax.ShapeDtypeStruct((W, W), BF)),
        in_specs=[smem, smem, hbm, hbm, hbm, hbm],
        out_specs=(vmem, vmem),
        scratch_shapes=scratch,
        compiler_params=pltpu.CompilerParams(
            collective_id=0, has_side_effects=True, vmem_limit_bytes=60 * 2**20
        ),
    )(tile_count[0], jnp.transpose(tile_col, (0, 3, 1, 2))[0], features, edge_tiles[0, 0], cotangent, weight)
    return activations, grad.astype(F32)


def solution(mesh):
    return jax.shard_map(
        local,
        mesh=mesh,
        in_specs=(
            P(("row", "col"), None),
            P(),
            P("row", "col", None, None, None, None),
            P("row", "col", None, None),
            P("row", "col", None),
            P(("row", "col"), None),
        ),
        out_specs=(P(("row", "col"), None), P()),
        check_vma=False,
    )
```

```python
import jax
import jax.numpy as jnp
from jax import lax
from jax.experimental import pallas as pl
from jax.experimental.pallas import tpu as pltpu
from jax.sharding import PartitionSpec as P

MESH = pl.DeviceIdType.MESH
BF, F32 = jnp.bfloat16, jnp.float32
N, W = 128, 512
CHUNKS = ((0, 128), (128, 128), (256, 128), (384, 128))
C = len(CHUNKS)
PIECES = tuple((f, r, 64) for f in range(C) for r in (0, 64))
NP = len(PIECES)


def of(step, f, first=1):
    return [(step, f, i) for i in range(first, 4)]


def pieces(step, f):
    return [(step, p) for p in range(NP) if PIECES[p][0] == f]


def mixed(*lists):
    return [each[i] for i in range(max(map(len, lists))) for each in lists if i < len(each)]


ORDER = [
    ("own", 0), ("line", 0), ("own", 1), ("line", 1), ("own", 2), ("line", 2), ("own", 3), ("line", 3),
    ("on", 0, 0), ("on", 1, 0), ("on", 2, 0), ("on", 3, 0),
    *of("ring", 0), *of("ring", 1), *of("on", 0), *of("ring", 2), *of("on", 1), *of("ring", 3),
    *of("end", 0, 0), *mixed(of("mul", 0, 0), of("on", 2)), *of("end", 1, 0), *mixed(of("mul", 1, 0), of("on", 3)),
    *pieces("y", 0), *of("end", 2, 0), *of("mul", 2, 0), *pieces("y", 1), *pieces("y_end", 0),
    *of("end", 3, 0), *of("mul", 3, 0), *pieces("y", 2), *pieces("y_end", 1), *pieces("z", 0),
    *pieces("y", 3), *pieces("y_end", 2), *pieces("y_end", 3), *pieces("z", 1), *pieces("z_end", 0),
    *pieces("z", 2), *pieces("z", 3), *pieces("z_end", 1), *pieces("z_end", 2), *pieces("z_end", 3),
]


def device(x, zl, k, zh, y):
    return ((x * 4 + zl) * 2 + k, zh * 4 + y)


def turn(value, by):
    return lax.rem(value + (by + 16), 4)


def far(offset):
    dx, dy = offset // 4, offset % 4
    return min(dx, 4 - dx) + min(dy, 4 - dy)


NEAR_FIRST = sorted(range(1, 16), key=far)


def kernel(
    count_ref, col_ref, feat, edges, cot, weight, act_out, grad_out,
    *scratch,
):
    ag, te = scratch[:C], scratch[C : 2 * C]
    r1, r2, su, sb, r3, r4 = (scratch[2 * C + i * NP : 2 * C + (i + 1) * NP] for i in range(6))
    (raw, em, cv, wv, av, gv, own, sib, rsib, part, rxy, hi, lo, gxy,
     in_sem, zs, zr, xs, xr, fs, fr, cs, cr, ys, yr, ys2, yr2, zs1, zr1, zs2, zr2, a_s, a_r, g_r) = scratch[2 * C + 6 * NP :]
    row, col = lax.axis_index("row"), lax.axis_index("col")
    x, zl, k = row // 8, lax.rem(row // 2, 4), lax.rem(row, 2)
    zh, y = col // 4, lax.rem(col, 4)
    sibling = device(x, zl, 1 - k, zh, y)
    right, left = device(turn(x, 1), zl, k, zh, y), device(turn(x, -1), zl, k, zh, y)
    up, down = device(x, zl, k, zh, turn(y, 1)), device(x, zl, k, zh, turn(y, -1))
    above, below = device(x, zl, k, turn(zh, 1), y), device(x, zl, k, turn(zh, -1), y)
    line = [device(x, turn(zl, d), k, zh, y) for d in (1, 2, 3)]
    first, last = 1 + lax.rem(zl, 2), 3 * (1 - zl // 2)
    places = (zl, first, 6 - zl - first - last, last)

    def slot(core, at_x, at_zl=0):
        return core * 16 + at_x * 4 + at_zl

    def send(src, dst, send_sem, recv_sem, to):
        pltpu.make_async_remote_copy(
            src_ref=src, dst_ref=dst, send_sem=send_sem, recv_sem=recv_sem, device_id=to, device_id_type=MESH
        ).start()

    def wait(ref, sem):
        pltpu.make_async_copy(ref, ref, sem).wait()

    loads = [
        pltpu.make_async_copy(feat.at[:, s : s + w], ag[f].at[slot(k, x, zl)], in_sem.at[f])
        for f, (s, w) in enumerate(CHUNKS)
    ]
    loads += [
        pltpu.make_async_copy(edges, raw, in_sem.at[C]),
        pltpu.make_async_copy(weight, wv, in_sem.at[C + 1]),
        pltpu.make_async_copy(cot, cv, in_sem.at[C + 2]),
    ]
    for load in loads:
        load.start()

    barrier = pltpu.get_barrier_semaphore()
    partners = [*line, above, below, right, left, up, down, sibling]
    for to in partners:
        pl.semaphore_signal(barrier, inc=1, device_id=to, device_id_type=MESH)
    pl.semaphore_wait(barrier, len(partners))

    def to_sibling(f, at_x):
        ref = ag[f].at[pl.ds(slot(k, at_x), 4)]
        send(ref, ref, cs.at[f], cr.at[f], sibling)

    def to_ring(f, i):
        ref = ag[f].at[slot(k, x, places[i])]
        send(ref, ref, xs.at[f], xr.at[f, 0, i], right)
        send(ref, ref, xs.at[f], xr.at[f, 1, i], left)
        if i == 3:
            to_sibling(f, x)

    def gather_own(f):
        loads[f].wait()
        to_ring(f, 0)

    def gather_line(f):
        ref = ag[f].at[slot(k, x, zl)]
        for to in line:
            send(ref, ref, zs.at[f], zr.at[f, zl], to)

    def gather_ring(f, i):
        ref = ag[f].at[slot(k, x, places[i])]
        wait(ref, zr.at[f, places[i]])
        to_ring(f, i)

    def gather_on(f, i):
        refs = [ag[f].at[slot(k, turn(x, d), places[i])] for d in (-1, 1)]
        for d in (i % 2, 1 - i % 2):
            wait(refs[d], xr.at[f, d, i])
            if d == i % 2:
                send(refs[d], refs[d], fs.at[f], fr.at[f, i], left if d else right)
            if i == 3:
                to_sibling(f, turn(x, (-1, 1)[d]))

    def gather_end(f, i):
        ref = ag[f].at[slot(k, turn(x, 2), places[i])]
        wait(ref, fr.at[f, i])
        if i == 3:
            to_sibling(f, turn(x, 2))

    def mask_tiles():
        loads[C].wait()

        def one(a, _):
            count = count_ref[0, a]
            for s in range(3):
                tile = raw[a, s]
                em[a, :, s * N : (s + 1) * N] = jnp.where(s < count, tile, jnp.zeros_like(tile))
            return _

        lax.fori_loop(0, 16, one, 0)

    def terms(f, to_y):
        for q in range(4):
            a = q * 4 + to_y
            picked = []
            for s in range(3):
                j = col_ref[s, 0, a]
                picked.append(ag[f][lax.rem(j, 2) * 16 + j // 2])
            made = jnp.dot(em[a], jnp.concatenate(picked, axis=0), preferred_element_type=F32)
            te[f][to_y * 4 + q] = made.astype(BF)

    y_up, y_down, y_far = turn(y, 1), turn(y, -1), turn(y, 2)

    def multiply(f, group):
        if group == 0:
            wait(ag[f].at[pl.ds(0, 16)], cr.at[f])
        terms(f, (y_far, y_up, y_down, y)[group])
        for p, (chunk, r, n) in enumerate(PIECES):
            rows = pl.ds(r, n)
            if chunk != f:
                continue
            if group == 0:
                send(te[f].at[pl.ds(y_far * 4, 2), rows], r1[p].at[0], ys.at[p], yr.at[p, 0], up)
                send(te[f].at[pl.ds(y_far * 4 + 2, 2), rows], r1[p].at[1], ys.at[p], yr.at[p, 1], down)
            if group == 1:
                send(te[f].at[pl.ds(y_up * 4 + 2, 2), rows], r2[p].at[0, pl.ds(2, 2)], ys2.at[p], yr2.at[p], up)
            if group == 2:
                send(te[f].at[pl.ds(y_down * 4, 2), rows], r2[p].at[1, pl.ds(0, 2)], ys2.at[p], yr2.at[p], down)

    def reduce_y(p):
        f, r, n = PIECES[p]
        for d, at, to in ((0, y_up * 4, up), (1, y_down * 4 + 2, down)):
            wait(r1[p].at[d], yr.at[p, d])
            ref = te[f].at[pl.ds(at, 2), pl.ds(r, n)]
            ref[...] = (ref[...].astype(F32) + r1[p][d].astype(F32)).astype(BF)
            send(ref, r2[p].at[d, pl.ds(2 * d, 2)], ys2.at[p], yr2.at[p], to)

    z_up, z_down, z_far = turn(zh, 1), turn(zh, -1), turn(zh, 2)

    def reduce_y_end(p):
        f, r, n = PIECES[p]
        wait(r2[p], yr2.at[p])

        def total(q):
            return te[f][y * 4 + q, r : r + n].astype(F32) + r2[p][0, q].astype(F32) + r2[p][1, q].astype(F32)

        sb[p][z_far] = total(z_far).astype(BF)
        send(sb[p].at[z_far, pl.ds(0, n // 2)], r3[p].at[0], zs1.at[p], zr1.at[p, 0], above)
        send(sb[p].at[z_far, pl.ds(n // 2, n // 2)], r3[p].at[1], zs1.at[p], zr1.at[p, 1], below)
        for q in (z_up, z_down, zh):
            su[p][q] = total(q)

    def reduce_z(p):
        h = PIECES[p][2] // 2
        for d, at, to in ((0, z_up, above), (1, z_down, below)):
            wait(r3[p].at[d], zr1.at[p, d])
            add, keep = pl.ds(d * h, h), pl.ds((1 - d) * h, h)
            sb[p][at, add] = (su[p][at, add] + r3[p][d].astype(F32)).astype(BF)
            sb[p][at, keep] = su[p][at, keep].astype(BF)
            send(sb[p].at[at], r4[p].at[d], zs2.at[p], zr2.at[p], to)

    def sent():
        for f in range(C):
            wait(ag[f].at[pl.ds(0, 3)], zs.at[f])
            wait(ag[f].at[pl.ds(0, 8)], xs.at[f])
            wait(ag[f].at[pl.ds(0, 4)], fs.at[f])
            wait(ag[f].at[pl.ds(0, 16)], cs.at[f])
        for p in range(NP):
            wait(r1[p], ys.at[p])
            wait(r2[p], ys2.at[p])

    def reduce_z_end(p):
        f, r, n = PIECES[p]
        s, w = CHUNKS[f]
        if p == 2:
            sent()
            loads[C + 1].wait()
            loads[C + 2].wait()
        wait(r4[p], zr2.at[p])
        av[r : r + n, s : s + w] = (su[p][zh] + r4[p][0].astype(F32) + r4[p][1].astype(F32)).astype(BF)

    steps = {
        "own": gather_own, "line": gather_line, "ring": gather_ring, "on": gather_on, "end": gather_end, "mul": multiply,
        "y": reduce_y, "y_end": reduce_y_end, "z": reduce_z, "z_end": reduce_z_end,
    }
    for step, *which in ORDER:
        if (step, *which) == ("on", 0, 0):
            mask_tiles()
        steps[step](*which)

    preact = jnp.dot(av[...], wv[...], preferred_element_type=F32)
    sig = jax.nn.sigmoid(preact)
    gv[...] = (cv[...].astype(F32) * sig * (1.0 + preact * (1.0 - sig))).astype(BF)
    act_out[...] = (preact * sig).astype(BF)

    def share(half):
        rows = av[:, pl.ds(pl.multiple_of(half * 256, 256), 256)]
        made = lax.dot_general(rows, gv[...], (((0,), (0,)), ((), ())), preferred_element_type=F32)
        return made.reshape(16, 16, W)

    sib[...] = share(1 - k).astype(BF)
    send(sib, rsib, a_s.at[0], a_r.at[0], sibling)
    own[...] = share(k)
    for p in range(NP):
        wait(r3[p], zs1.at[p])
        wait(r4[p], zs2.at[p])
    wait(rsib, a_r.at[0])

    place = x * 4 + y

    def peer(i):
        return turn(x, i // 4), turn(y, i % 4)

    for i in reversed(NEAR_FIRST):
        px, py = peer(i)
        part[px * 4 + py] = (own[px * 4 + py] + rsib[px * 4 + py].astype(F32)).astype(BF)
        send(part.at[px * 4 + py], rxy.at[i - 1], a_s.at[1], a_r.at[1], device(px, zl, k, zh, py))
    wait(rxy, a_r.at[1])
    total = own[place] + rsib[place].astype(F32)
    for i in range(15):
        total = total + rxy[i].astype(F32)

    def exchange(buf, at, stage, to):
        buf[at] = total.astype(BF)
        for d in (2, 1, 3):
            send(buf.at[at], buf.at[at], a_s.at[stage], a_r.at[stage], to(d))
        wait(buf.at[pl.ds(0, 3)], a_r.at[stage])
        return sum(buf[i].astype(F32) for i in range(4))

    total = exchange(lo, zl, 3, lambda d: line[d - 1])
    total = exchange(hi, zh, 2, lambda d: device(x, zl, k, turn(zh, d), y))

    here = k * 16 + place
    gxy[here] = total.astype(BF)
    send(gxy.at[here], gxy.at[here], a_s.at[5], a_r.at[5], sibling)
    for i in reversed(NEAR_FIRST):
        px, py = peer(i)
        send(gxy.at[here], gxy.at[here], a_s.at[4], g_r.at[i], device(px, zl, k, zh, py))
    for i in NEAR_FIRST:
        ref = gxy.at[k * 16 + turn(x, -(i // 4)) * 4 + turn(y, -(i % 4))]
        wait(ref, g_r.at[i])
        send(ref, ref, a_s.at[5], a_r.at[5], sibling)

    wait(sib, a_s.at[0])
    wait(rxy, a_s.at[1])
    wait(hi.at[pl.ds(0, 3)], a_s.at[2])
    wait(lo.at[pl.ds(0, 3)], a_s.at[3])
    wait(rxy, a_s.at[4])
    wait(part, a_s.at[5])
    wait(part, a_r.at[5])
    grad_out[...] = gxy[...].reshape(W, W)


def local(features, weight, edge_tiles, tile_col, tile_count, cotangent):
    vm = pltpu.VMEM
    scratch = []
    for rows in (32, 16):
        scratch += [vm((rows, N, w), BF) for _, w in CHUNKS]
    for shape, part, kind in (((2, 2), 1, BF), ((2, 4), 1, BF), ((4,), 1, F32), ((4,), 1, BF), ((2,), 2, BF), ((2,), 1, BF)):
        scratch += [vm((*shape, n // part, CHUNKS[f][1]), kind) for f, _, n in PIECES]
    scratch += [
        vm((16, 3, N, N), BF), vm((16, N, 3 * N), BF), vm((N, W), BF), vm((W, W), BF), vm((N, W), BF), vm((N, W), BF),
        vm((16, 16, W), F32), vm((16, 16, W), BF), vm((16, 16, W), BF), vm((16, 16, W), BF), vm((15, 16, W), BF),
        vm((4, 16, W), BF), vm((4, 16, W), BF), vm((32, 16, W), BF),
    ]
    for shape in (
        (C + 3,), (C,), (C, 4), (C,), (C, 2, 4), (C,), (C, 4), (C,), (C,),
        (NP,), (NP, 2), (NP,), (NP,), (NP,), (NP, 2), (NP,), (NP,), (6,), (6,), (16,),
    ):
        scratch.append(pltpu.SemaphoreType.DMA(shape))
    smem, hbm, vmem = (pl.BlockSpec(memory_space=m) for m in (pltpu.SMEM, pltpu.HBM, pltpu.VMEM))
    activations, grad = pl.pallas_call(
        kernel,
        name="conv",
        out_shape=(jax.ShapeDtypeStruct((N, W), BF), jax.ShapeDtypeStruct((W, W), BF)),
        in_specs=[smem, smem, hbm, hbm, hbm, hbm],
        out_specs=(vmem, vmem),
        scratch_shapes=scratch,
        compiler_params=pltpu.CompilerParams(
            collective_id=0, has_side_effects=True, vmem_limit_bytes=60 * 2**20
        ),
    )(tile_count[0], jnp.transpose(tile_col, (0, 3, 1, 2))[0], features, edge_tiles[0, 0], cotangent, weight)
    return activations, grad.astype(F32)


def solution(mesh):
    return jax.shard_map(
        local,
        mesh=mesh,
        in_specs=(
            P(("row", "col"), None),
            P(),
            P("row", "col", None, None, None, None),
            P("row", "col", None, None),
            P("row", "col", None),
            P(("row", "col"), None),
        ),
        out_specs=(P(("row", "col"), None), P()),
        check_vma=False,
    )
```
